128 devices in a mesh: patch: 32 (over z, x, core), feat: 4 (over y).
Axes of the slice: x: 4, y: 4, z: 4, core: 2. Of those that a mesh axis runs over, the one named last changes fastest.
Arguments:
- node_latents: bfloat16 [16384, 512], P('patch'), may hold values from -6 to 6
- edge_latents: bfloat16 [131072, 512], P('patch'), may hold values from -6 to 6
- send_rows: int32 [32, 32, 128], P('patch'), may hold values from 0 to 511, as said below
- edge_slot: int32 [131072], P('patch'), may hold values from 0 to 4095, as said below
- receivers: int32 [131072], P('patch'), may hold values from 0 to 511
- edge_in_w: bfloat16 [3, 3, 512, 512], P(None, None, None, 'feat'), may hold values from -0.15625 to 0.15625
- edge_in_b: float32 [3, 512], P(None, 'feat'), may hold values from -3 to 3
- edge_out_w: bfloat16 [3, 512, 512], P(None, 'feat'), may hold values from -0.25 to 0.25
- edge_gain: float32 [3, 512], replicated, may hold values from 0.5 to 2
- node_in_w: bfloat16 [3, 2, 512, 512], P(None, None, None, 'feat'), may hold values from -0.1875 to 0.1875
- node_in_b: float32 [3, 512], P(None, 'feat'), may hold values from -3 to 3
- node_out_w: bfloat16 [3, 512, 512], P(None, 'feat'), may hold values from -0.25 to 0.25
- node_gain: float32 [3, 512], replicated, may hold values from 0.5 to 2
Outputs:
- node_state: bfloat16 [16384, 512], P('patch')
- edge_state: bfloat16 [131072, 512], P('patch')
The draws below stay inside these ranges and needn't reach their ends.
Inputs may be any that keep to these rules, and one draw needn't show every extreme that they name: `send_rows`: the rows that one pair (s, d) names at slots used by some edge are distinct; unused slots hold 0. Every edge of patch d names a used slot of some patch s. Each patch names its last node row in the first slot it provides to itself. `edge_slot`: every patch holds exactly 4096 edges, all ending at its own nodes.
All inputs are finite; a program needn't handle non-finite values.
Results may differ from the reference program's by a relative error of at most 0.023.
Values may be sent and summed in bfloat16 or wider, within the bound.
No kernel may reach another device: no remote copies, remote signals or barrier semaphores. Data moves between devices by JAX's collectives and lax.ppermute only.
A program may use at most 128 MiB of HBM per device.

```python
import math
import jax
import jax.numpy as jnp
from jax import lax

D = 512
H = 512
NODE_DEV = 512
LAYERS = 3
EDGE_DEV = 4096
CAP = 128
PEERS = 32
NODES = 16384
EDGES = 131072
N_FEAT = 4


def route_plan(key):
    count_key = jax.random.fold_in(key, 101)
    row_key = jax.random.fold_in(key, 102)
    edge_key = jax.random.fold_in(key, 103)
    source_idx = jnp.arange(PEERS, dtype=jnp.int32)[:, None]
    target_idx = jnp.arange(PEERS, dtype=jnp.int32)[None, :]
    apart_gap = jnp.abs(source_idx - target_idx)
    cycle_gap = jnp.minimum(apart_gap, PEERS - apart_gap)
    sparse_counts = jax.random.randint(count_key, (PEERS, PEERS), max(CAP // 8, 1), CAP // 2 + 1)
    counts = jnp.where(cycle_gap <= 2, CAP, sparse_counts)
    row_keys = jax.random.split(row_key, PEERS * PEERS)

    def pick_rows(subkey):
        return jax.random.permutation(subkey, NODE_DEV)[:CAP]
    chosen = jax.vmap(pick_rows)(row_keys).reshape(PEERS, PEERS, CAP).astype(jnp.int32)
    leading = chosen[:, :, 0:1]
    rotated = (chosen + (NODE_DEV - 1) - leading) % NODE_DEV
    on_diag = (source_idx == target_idx)[:, :, None]
    chosen = jnp.where(on_diag, rotated, chosen).astype(jnp.int32)
    in_use = jnp.arange(CAP, dtype=jnp.int32)[None, None, :] < counts[:, :, None]
    row_table = jnp.where(in_use, chosen, 0).astype(jnp.int32)
    return (in_use, row_table, edge_key)


def edges_for(used_flat, subkey):
    ordering = jnp.argsort(jnp.where(used_flat, 0, 1).astype(jnp.int32), stable=True).astype(jnp.int32)
    live_count = jnp.sum(used_flat.astype(jnp.int32))
    pick_key, shuffle_key = jax.random.split(subkey)
    extra_pick = jax.random.randint(pick_key, (EDGE_DEV,), 0, live_count)
    positions = jnp.arange(EDGE_DEV, dtype=jnp.int32)
    picked = jnp.where(positions < live_count, positions, extra_pick)
    slot_list = ordering[picked]
    return jax.random.permutation(shuffle_key, slot_list)


def draw_send_rows(key, part):
    in_use, row_table, edge_key = route_plan(key)
    return row_table


def draw_edge_slot(key, part):
    in_use, row_table, edge_key = route_plan(key)
    per_target = jnp.transpose(in_use, (1, 0, 2)).reshape(PEERS, PEERS * CAP)
    target_keys = jax.random.split(edge_key, PEERS)
    slot_table = jax.vmap(edges_for)(per_target, target_keys)
    return slot_table.reshape(-1).astype(jnp.int32)


def set_ends(entries, rng, low, largest):
    longest = entries.shape.index(max(entries.shape))
    spots = []
    for shift in (0, 1):
        where = [jax.random.randint(jax.random.fold_in(rng, axis), (), 0, length) for axis, length in enumerate(entries.shape)]
        where[longest] = (where[longest] + shift) % entries.shape[longest]
        spots.append(tuple(where))
    return entries.at[spots[0]].set(low).at[spots[1]].set(largest)


def shard_levels(rng, dims, pieces, least, top_value):
    def one(dim, shards_of):
        draws = jax.random.uniform(jax.random.fold_in(jax.random.fold_in(rng, 6), dim), (shards_of,), jnp.float32, least / len(pieces), top_value / len(pieces))
        return jnp.repeat(jnp.exp(draws), dims[dim] // shards_of).reshape((-1,) + (1,) * (len(dims) - dim - 1))

    factor_of = one(*pieces[0])
    for cut in pieces[1:]:
        factor_of = factor_of * one(*cut)
    return factor_of


def centred(rng, dims, scale, bound, cuts=(), kind=jnp.bfloat16):
    entries = jax.random.normal(rng, dims, jnp.float32) * scale
    if len(cuts) > 0:
        entries = shard_levels(rng, dims, cuts, -0.22, 0.18) * entries
    return jnp.clip(entries, min=-bound, max=bound).astype(kind)


def setup_inputs(seed: int = 0) -> dict:
    keys = jax.random.split(jax.random.key(seed), 14)
    return {
        "node_latents": centred(keys[0], (NODES, D), 1.0, 6.0, ((0, 32),)),
        "edge_latents": centred(keys[1], (EDGES, D), 1.0, 6.0, ((0, 32),)),
        "send_rows": draw_send_rows(jax.random.fold_in(keys[13], 71), 0),
        "edge_slot": draw_edge_slot(jax.random.fold_in(keys[13], 71), 0),
        "receivers": set_ends(jax.random.randint(keys[4], (EDGES,), 0, NODE_DEV), jax.random.fold_in(keys[4], 1), 0, NODE_DEV - 1).astype(jnp.int32),
        "edge_in_w": centred(keys[5], (LAYERS, 3, D, H), (3 * D) ** -0.5, 0.15625, ((3, 4),)),
        "edge_in_b": centred(keys[6], (LAYERS, H), 0.5, 3.0, ((1, 4),), jnp.float32),
        "edge_out_w": centred(keys[7], (LAYERS, H, D), H ** -0.5, 0.25, ((1, 4),)),
        "edge_gain": jnp.clip(jnp.exp(jax.random.uniform(keys[8], (LAYERS, D), jnp.float32, math.log(0.5), math.log(2.0))), 0.5, 2.0),
        "node_in_w": centred(keys[9], (LAYERS, 2, D, H), (2 * D) ** -0.5, 0.1875, ((3, 4),)),
        "node_in_b": centred(keys[10], (LAYERS, H), 0.5, 3.0, ((1, 4),), jnp.float32),
        "node_out_w": centred(keys[11], (LAYERS, H, D), H ** -0.5, 0.25, ((1, 4),)),
        "node_gain": jnp.clip(jnp.exp(jax.random.uniform(keys[12], (LAYERS, D), jnp.float32, math.log(0.5), math.log(2.0))), 0.5, 2.0),
    }


def layer_norm(values, scales):
    center = values - lax.optimization_barrier(jnp.mean(values, axis=-1, keepdims=True))
    spread = lax.optimization_barrier(jnp.mean(center * center, axis=-1, keepdims=True))
    return center * lax.rsqrt(spread + 1e-05) * scales

def split_sum(hidden, weight):
    share_width = weight.shape[0] // N_FEAT
    running = jnp.zeros((hidden.shape[0], weight.shape[1]), jnp.float32)
    for feat_idx in range(N_FEAT):
        first = feat_idx * share_width
        partial_value = jnp.dot(hidden[:, first:first + share_width], weight[first:first + share_width], preferred_element_type=jnp.float32)
        rounded = lax.optimization_barrier(partial_value.astype(jnp.bfloat16))
        running = running + rounded.astype(jnp.float32)
    return running

def reference(node_latents, edge_latents, send_rows, edge_slot, receivers, edge_in_w, edge_in_b, edge_out_w, edge_gain, node_in_w, node_in_b, node_out_w, node_gain):
    slot_table = edge_slot.reshape(PEERS, EDGE_DEV)
    source = (slot_table // CAP).astype(jnp.int32)
    offset = (slot_table % CAP).astype(jnp.int32)
    target = jnp.arange(PEERS, dtype=jnp.int32)[:, None]
    local_rows = send_rows[source, target, offset]
    senders = (source * NODE_DEV + local_rows).reshape(-1).astype(jnp.int32)
    targets = (target * NODE_DEV + receivers.reshape(PEERS, EDGE_DEV)).reshape(-1).astype(jnp.int32)
    node_state = node_latents
    edge_state = edge_latents
    for layer_idx in range(LAYERS):
        sender_proj = jnp.dot(node_state, edge_in_w[layer_idx, 1], preferred_element_type=jnp.float32).astype(jnp.bfloat16)
        receiver_proj = jnp.dot(node_state, edge_in_w[layer_idx, 2], preferred_element_type=jnp.float32).astype(jnp.bfloat16)
        preact = jnp.dot(edge_state, edge_in_w[layer_idx, 0], preferred_element_type=jnp.float32)
        preact = preact + sender_proj[senders].astype(jnp.float32) + receiver_proj[targets].astype(jnp.float32) + edge_in_b[layer_idx]
        edge_hidden = jax.nn.silu(preact).astype(jnp.bfloat16)
        message = layer_norm(split_sum(edge_hidden, edge_out_w[layer_idx]), edge_gain[layer_idx])
        update = message.astype(jnp.bfloat16)
        edge_next = (edge_state.astype(jnp.float32) + message).astype(jnp.bfloat16)
        incoming = jax.ops.segment_sum(update.astype(jnp.float32), targets, num_segments=PEERS * NODE_DEV).astype(jnp.bfloat16)
        node_pre = jnp.dot(node_state, node_in_w[layer_idx, 0], preferred_element_type=jnp.float32)
        node_pre = node_pre + jnp.dot(incoming, node_in_w[layer_idx, 1], preferred_element_type=jnp.float32) + node_in_b[layer_idx]
        node_hidden = jax.nn.silu(node_pre).astype(jnp.bfloat16)
        node_change = layer_norm(split_sum(node_hidden, node_out_w[layer_idx]), node_gain[layer_idx])
        node_state = (node_state.astype(jnp.float32) + node_change).astype(jnp.bfloat16)
        edge_state = edge_next
    return (node_state, edge_state)
```

```python
import functools

import jax
import jax.numpy as jnp
from jax import lax
from jax.experimental import pallas as pl
from jax.experimental.pallas import tpu as pltpu
from jax.sharding import PartitionSpec as P

LAYERS = 3
CHUNKS = 2
BLOCK = 512
BF16 = jnp.bfloat16
F32 = jnp.float32
BIAS_ROWS = 16


def mm(a, b):
    return jnp.dot(a, b, preferred_element_type=F32)


def silu(v):
    half = 0.5 * v
    return half + half * jnp.tanh(half)


def norm(values, gain):
    center = values - jnp.mean(values, axis=-1, keepdims=True)
    spread = jnp.mean(center * center, axis=-1, keepdims=True)
    return center * lax.rsqrt(spread + 1e-05) * gain


def params():
    return pltpu.CompilerParams(vmem_limit_bytes=58 * 1024 * 1024)


def bundle_kernel(layer, ein_ref, eout_ref, nin_ref, nout_ref, nb_ref, out_ref):
    d, w = ein_ref.shape
    parts = d // w
    out_ref[0:d] = ein_ref[...]
    for j in range(parts):
        out_ref[d + j * w : d + (j + 1) * w] = eout_ref[:, j * w : (j + 1) * w]
        out_ref[4 * d + j * w : 4 * d + (j + 1) * w] = nout_ref[:, j * w : (j + 1) * w]
    out_ref[2 * d : 3 * d] = nin_ref[0]
    out_ref[3 * d : 4 * d] = nin_ref[1]
    bias = nb_ref[layer : layer + 1, :]
    first = bias.astype(BF16).astype(F32)
    second = (bias - first).astype(BF16).astype(F32)
    third = bias - first - second
    row = lax.broadcasted_iota(jnp.int32, (BIAS_ROWS, w), 0)
    terms = jnp.where(row == 0, first, jnp.where(row == 1, second, jnp.where(row == 2, third, 0.0)))
    out_ref[5 * d : 5 * d + BIAS_ROWS] = terms.astype(BF16)


def bundle(layer, edge_in_w, edge_out_w, node_in_w, node_out_w, node_in_b):
    d, w = edge_in_w.shape[2:]
    rows = 5 * d + BIAS_ROWS
    return pl.pallas_call(
        functools.partial(bundle_kernel, layer),
        grid=(1,),
        out_shape=jax.ShapeDtypeStruct((rows, w), BF16),
        in_specs=[
            pl.BlockSpec((None, None, d, w), lambda i: (layer, 0, 0, 0)),
            pl.BlockSpec((None, w, d), lambda i: (layer, 0, 0)),
            pl.BlockSpec((None, 2, d, w), lambda i: (layer, 0, 0, 0)),
            pl.BlockSpec((None, w, d), lambda i: (layer, 0, 0)),
            pl.BlockSpec(node_in_b.shape, lambda i: (0, 0)),
        ],
        out_specs=pl.BlockSpec((rows, w), lambda i: (0, 0)),
        compiler_params=params(),
        name="bundle",
    )(edge_in_w, edge_out_w, node_in_w, node_out_w, node_in_b)


def project(layer, state, ws_ref, wr_ref, eb_ref, rows_ref, slots_ref, recv_ref):
    sender = mm(state, ws_ref[...]).astype(BF16)
    recv_ref[...] = mm(state, wr_ref[...]) + eb_ref[layer : layer + 1, :]
    n = state.shape[0]
    peers, width = rows_ref.shape
    lanes = lax.broadcasted_iota(jnp.int32, (width, width), 1)

    def one(p, carry):
        index = jnp.broadcast_to(rows_ref[pl.ds(p, 1), :], (width, width)).T
        hot = jnp.concatenate(
            [jnp.where(index == lanes + j * width, 1.0, 0.0).astype(BF16) for j in range(n // width)], axis=1
        )
        slots_ref[pl.ds(p, 1)] = mm(hot, sender).astype(BF16)[None]
        return carry

    lax.fori_loop(0, peers, one, 0, unroll=4)


def first_kernel(node_ref, ws_ref, wr_ref, eb_ref, rows_ref, slots_ref, recv_ref):
    project(0, node_ref[...], ws_ref, wr_ref, eb_ref, rows_ref, slots_ref, recv_ref)


def project_specs(layer, edge_in_w, edge_in_b, send_rows):
    d, w = edge_in_w.shape[2:]
    return [
        pl.BlockSpec((None, None, d, w), lambda i: (layer, 1, 0, 0)),
        pl.BlockSpec((None, None, d, w), lambda i: (layer, 2, 0, 0)),
        pl.BlockSpec(edge_in_b.shape, lambda i: (0, 0)),
        pl.BlockSpec((None,) + send_rows.shape[1:], lambda i: (0, 0, 0)),
    ]


def project_outs(n, w, send_rows):
    peers, width = send_rows.shape[1:]
    shapes = [jax.ShapeDtypeStruct((peers, width, w), BF16), jax.ShapeDtypeStruct((n, w), F32)]
    specs = [pl.BlockSpec((peers, width, w), lambda i: (0, 0, 0)), pl.BlockSpec((n, w), lambda i: (0, 0))]
    return shapes, specs


def first(node_state, edge_in_w, edge_in_b, send_rows):
    n = node_state.shape[0]
    shapes, specs = project_outs(n, edge_in_w.shape[3], send_rows)
    return pl.pallas_call(
        first_kernel,
        grid=(1,),
        out_shape=shapes,
        in_specs=[pl.BlockSpec(node_state.shape, lambda i: (0, 0))]
        + project_specs(0, edge_in_w, edge_in_b, send_rows),
        out_specs=specs,
        compiler_params=params(),
        name="first",
    )(node_state, edge_in_w, edge_in_w, edge_in_b, send_rows)


def pick_kernel(start, slot_ref, recv_ref, table_ref, proj_ref, out_ref, wide_ref, acc_ref):
    wide_ref[...] = table_ref[...].astype(F32)
    group = 16

    def some(i, carry):
        base = i * group
        for r in range(group):
            s = slot_ref[start + base + r]
            q = recv_ref[start + base + r]
            acc_ref[pl.ds(base + r, 1), :] = wide_ref[pl.ds(s, 1), :] + proj_ref[pl.ds(q, 1), :]
        return carry

    lax.fori_loop(0, out_ref.shape[0] // group, some, 0)
    out_ref[...] = acc_ref[...].astype(BF16)


def pick(chunk, count, edge_slot, receivers, table, proj):
    w = table.shape[1]
    return pl.pallas_call(
        functools.partial(pick_kernel, chunk * count),
        grid=(1,),
        out_shape=jax.ShapeDtypeStruct((count, w), BF16),
        in_specs=[
            pl.BlockSpec(memory_space=pltpu.SMEM),
            pl.BlockSpec(memory_space=pltpu.SMEM),
            pl.BlockSpec(table.shape, lambda i: (0, 0)),
            pl.BlockSpec(proj.shape, lambda i: (0, 0)),
        ],
        out_specs=pl.BlockSpec((count, w), lambda i: (0, 0)),
        scratch_shapes=[pltpu.VMEM(table.shape, F32), pltpu.VMEM((count, w), F32)],
        compiler_params=params(),
        name="pick",
    )(edge_slot, receivers, table, proj)


def edge_kernel(layer, chunk, blocks, more, *refs):
    refs = list(refs)

    def take(k):
        got = refs[:k]
        del refs[:k]
        return got

    (x_ref,) = take(1)
    pre_refs = take(4)
    weight_refs = take(4)
    recv_ref, gain_ref = take(2)
    last_chunk = chunk == CHUNKS - 1
    if chunk > 0:
        _, before_ref = take(2)
    if last_chunk:
        node_ref, ngain_ref = take(2)
        nw_refs = [take(4) for _ in range(4)]
        if more:
            proj_in = take(4)
    (edge_out_ref,) = take(1)
    if last_chunk:
        (node_out_ref,) = take(1)
        if more:
            proj_out = take(2)
    else:
        (sum_ref,) = take(1)
    w0_ref, w1_ref = take(2)
    if last_chunk:
        (sum_ref,) = take(1)

    step = pl.program_id(0)
    w = pre_refs[0].shape[1]
    d = x_ref.shape[1]

    @pl.when(step == 0)
    def _():
        for j, ref in enumerate(weight_refs):
            w0_ref[:, j * w : (j + 1) * w] = ref[0:d]
            for k in range(d // w):
                w1_ref[j * w : (j + 1) * w, k * w : (k + 1) * w] = ref[d + k * w : d + (k + 1) * w]
        if chunk > 0:
            sum_ref[...] = before_ref[...]
        else:
            sum_ref[...] = jnp.zeros_like(sum_ref)

    x = x_ref[...]
    extra = jnp.concatenate([ref[...] for ref in pre_refs], axis=1).astype(F32)
    hidden = silu(mm(x, w0_ref[...]) + extra).astype(BF16)
    message = norm(mm(hidden, w1_ref[...]), gain_ref[layer : layer + 1, :])
    edge_out_ref[...] = (x.astype(F32) + message).astype(BF16)
    n = sum_ref.shape[0]
    ids = lax.broadcasted_iota(jnp.int32, (n, x.shape[0]), 0)
    hot = jnp.where(ids == recv_ref[...], 1.0, 0.0).astype(BF16)
    sum_ref[...] += mm(hot, message.astype(BF16))

    if last_chunk:

        @pl.when(step == blocks - 1)
        def _():
            node = node_ref[...]
            incoming = sum_ref[...].astype(BF16)
            for j in range(4):
                w0_ref[:, j * w : (j + 1) * w] = nw_refs[0][j][...]
                w1_ref[:, j * w : (j + 1) * w] = nw_refs[1][j][...]
            bias = jnp.concatenate(
                [jnp.sum(nw_refs[3][j][...].astype(F32), axis=0, keepdims=True) for j in range(4)], axis=1
            )
            node_hidden = silu(mm(node, w0_ref[...]) + mm(incoming, w1_ref[...]) + bias).astype(BF16)
            for j in range(4):
                for k in range(d // w):
                    w0_ref[j * w : (j + 1) * w, k * w : (k + 1) * w] = nw_refs[2][j][k * w : (k + 1) * w]
            change = norm(mm(node_hidden, w0_ref[...]), ngain_ref[layer : layer + 1, :])
            state = (node.astype(F32) + change).astype(BF16)
            node_out_ref[...] = state
            if more:
                project(layer + 1, state, *proj_in, *proj_out)


def edges(layer, chunk, edge_state, pres, bundles, receivers, edge_gain, carried, node_args, proj_args):
    total, d = edge_state.shape
    count = total // CHUNKS
    blocks = count // BLOCK
    base = chunk * blocks
    w = pres[0].shape[1]
    last_chunk = chunk == CHUNKS - 1
    more = proj_args is not None
    whole = lambda a: pl.BlockSpec(a.shape, lambda i: (0,) * a.ndim)
    args = [edge_state, *pres, *bundles, receivers, edge_gain]
    specs = [pl.BlockSpec((BLOCK, d), lambda i: (base + i, 0))]
    specs += [pl.BlockSpec((BLOCK, w), lambda i: (i, 0))] * 4
    specs += [pl.BlockSpec((2 * d, w), lambda i: (0, 0))] * 4
    specs += [pl.BlockSpec((1, BLOCK), lambda i: (0, base + i)), whole(edge_gain)]
    aliases = {}
    if chunk > 0:
        aliases = {len(args): 0}
        args += list(carried)
        specs += [pl.BlockSpec(memory_space=pl.ANY), whole(carried[1])]
    shapes = [jax.ShapeDtypeStruct((total, d), BF16)]
    outs = [pl.BlockSpec((BLOCK, d), lambda i: (base + i, 0))]
    n = node_args[0].shape[0]
    scratch = [pltpu.VMEM((d, d), BF16), pltpu.VMEM((d, d), BF16)]
    if last_chunk:
        node_state, node_gain = node_args
        args += [node_state, node_gain]
        specs += [whole(node_state), whole(node_gain)]
        for part in range(2, 5):
            args += list(bundles)
            specs += [pl.BlockSpec((d, w), lambda i, part=part: (part, 0))] * 4
        args += list(bundles)
        specs += [pl.BlockSpec((BIAS_ROWS, w), lambda i: (5 * d // BIAS_ROWS, 0))] * 4
        shapes.append(jax.ShapeDtypeStruct((n, d), BF16))
        outs.append(pl.BlockSpec((n, d), lambda i: (0, 0)))
        if more:
            edge_in_w, edge_in_b, send_rows = proj_args
            args += [edge_in_w, edge_in_w, edge_in_b, send_rows]
            specs += project_specs(layer + 1, edge_in_w, edge_in_b, send_rows)
            more_shapes, more_specs = project_outs(n, w, send_rows)
            shapes += more_shapes
            outs += more_specs
        scratch.append(pltpu.VMEM((n, d), F32))
    else:
        shapes.append(jax.ShapeDtypeStruct((n, d), F32))
        outs.append(pl.BlockSpec((n, d), lambda i: (0, 0)))
    return pl.pallas_call(
        functools.partial(edge_kernel, layer, chunk, blocks, more),
        grid=(blocks,),
        out_shape=shapes,
        in_specs=specs,
        out_specs=outs,
        scratch_shapes=scratch,
        input_output_aliases=aliases,
        compiler_params=params(),
        name="edges",
    )(*args)


def body(
    node_latents,
    edge_latents,
    send_rows,
    edge_slot,
    receivers,
    edge_in_w,
    edge_in_b,
    edge_out_w,
    edge_gain,
    node_in_w,
    node_in_b,
    node_out_w,
    node_gain,
):
    feat = lax.axis_size("feat")
    count = edge_latents.shape[0] // CHUNKS
    receiver_row = receivers.reshape(1, -1)

    def shift(value, by):
        return lax.ppermute(value, "feat", [(i, (i + by) % feat) for i in range(feat)])

    def gathered(layer):
        own = bundle(layer, edge_in_w, edge_out_w, node_in_w, node_out_w, node_in_b)
        return own

    edge_state = edge_latents
    node_state = node_latents
    slots, recv_proj = first(node_state, edge_in_w, edge_in_b, send_rows)
    for layer in range(LAYERS):
        own = bundle(layer, edge_in_w, edge_out_w, node_in_w, node_out_w, node_in_b)
        slots, own = lax.optimization_barrier((slots, own))
        bundles = (own, shift(own, 1), shift(own, -1), shift(own, 2))
        table = lax.all_to_all(slots, "patch", split_axis=0, concat_axis=0, tiled=True)
        table = table.reshape(-1, table.shape[2])
        near = []
        for chunk in range(CHUNKS):
            mine = pick(chunk, count, edge_slot, receivers, table, recv_proj)
            left, right = shift(mine, 1), shift(mine, -1)
            far = shift(left, 1) if chunk % 2 == 0 else shift(right, -1)
            near.append((mine, left, right, far))
        carried = None
        for chunk in range(CHUNKS):
            last = chunk == CHUNKS - 1
            proj_args = (edge_in_w, edge_in_b, send_rows) if last and layer < LAYERS - 1 else None
            carried = edges(
                layer, chunk, edge_state, near[chunk], bundles, receiver_row, edge_gain, carried,
                (node_state, node_gain), proj_args,
            )
        if layer < LAYERS - 1:
            edge_state, node_state, slots, recv_proj = carried
        else:
            edge_state, node_state = carried
    return (node_state, edge_state)


def solution(mesh):
    in_specs = (
        P("patch", None),
        P("patch", None),
        P("patch", None, None),
        P("patch"),
        P("patch"),
        P(None, None, None, "feat"),
        P(None, "feat"),
        P(None, "feat", None),
        P(),
        P(None, None, None, "feat"),
        P(None, "feat"),
        P(None, "feat", None),
        P(),
    )
    out_specs = (P("patch", None), P("patch", None))
    return jax.shard_map(body, mesh=mesh, in_specs=in_specs, out_specs=out_specs, check_vma=False)
```
